32 devices in a mesh: dev: 32 (over z, y, x, core).
Axes of the slice: x: 2, y: 2, z: 4, core: 2. Of those that a mesh axis runs over, the one named last changes fastest.
Arguments:
- coefficients: bfloat16 [128, 4, 128, 128], P('dev'), may hold values from -6 to 6
- send_tile: int32 [32, 32], P('dev'), may hold values from 0 to 3
- slot_external: int32 [32, 32], P('dev'), may hold values from 0 to 7
- slot_pairs: int32 [32, 32, 3], P('dev'), may hold values from 0 to 63
- factor_alpha: bfloat16 [64, 128, 128], replicated, may hold values from -0.5 to 0.5
- factor_beta: bfloat16 [64, 128, 128], replicated, may hold values from -0.5 to 0.5
- denominators: float32 [256, 4, 128, 128], P('dev'), may hold values from 4 to 32
Outputs:
- amplitudes: bfloat16 [256, 4, 128, 128], P('dev')
- dressing: float32 [128, 4, 128, 128], P('dev')
- gram: float32 [4, 4], replicated
The draws below stay inside these ranges and needn't reach their ends.
All inputs are finite; a program needn't handle non-finite values.
Results may differ from the reference program's by a relative error of at most 0.004.
The reference program's roundings to bfloat16 on the way count: a program that leaves them out, or rounds other values in their place, can miss the bound.
Values may be sent and summed in bfloat16 or wider, within the bound.
No kernel may reach another device: no remote copies, remote signals or barrier semaphores. Data moves between devices by JAX's collectives and lax.ppermute only.
A program may use at most 128 MiB of HBM per device.

```python
import math
import jax
import jax.numpy as jnp
import numpy as np
from jax import lax

S = 4
A = 128
V_DEV = 4
E_DEV = 8
J = 3
P_SIZE = 64
VT = 128
ET = 256
N_DEV = 32


def touch_ends(entries, stream_key, low, high):
    shape = entries.shape
    spot = [jax.random.randint(jax.random.fold_in(stream_key, axis), (), 0, shape[axis]) for axis in range(len(shape))]
    entries = entries.at[tuple(spot)].set(low)
    longest = shape.index(max(shape))
    spot[longest] = (spot[longest] + 1) % shape[longest]
    return entries.at[tuple(spot)].set(high)


def shard_levels(own_key, dims, pieces, least, top_value):
    factor_of, own = 1.0, jax.random.fold_in(own_key, 6)
    for axis_at, blocks in pieces:
        heights = jnp.exp(jax.random.uniform(jax.random.fold_in(own, axis_at), (blocks,), jnp.float32, least / len(pieces), top_value / len(pieces)))
        factor_of = factor_of * jnp.repeat(heights, dims[axis_at] // blocks).reshape([-1 if axis == axis_at else 1 for axis in range(len(dims))])
    return factor_of


def cumulative_ranks(number_of, slope):
    portions = [(1 << 20) // math.isqrt(grade ** slope) + 1 for grade in range(1, number_of + 1)]
    spread = 1 + sum(portions) // (1 << 30)
    return np.cumsum(np.array([max(1, weight // spread) for weight in portions]))


def ranked(rng, extent, number_of, skew):
    table = cumulative_ranks(number_of, skew)
    lot = jax.random.randint(jax.random.fold_in(rng, 1), extent, 0, int(table[number_of - 1]))
    rank = jnp.searchsorted(jnp.asarray(table, jnp.int32), lot, side="right")
    return jax.random.permutation(jax.random.fold_in(rng, 2), number_of)[rank].astype(jnp.int32)


def bell_draw(rng, dims, spread, limit, cuts=(), kind=jnp.bfloat16):
    result = jax.random.normal(rng, dims, jnp.float32) * spread
    if len(cuts) > 0:
        result = shard_levels(rng, dims, cuts, -0.22, 0.18) * result
    return jnp.clip(result, min=-limit, max=limit).astype(kind)


def setup_inputs(seed: int = 0) -> dict:
    streams_of = jax.random.split(jax.random.key(seed), 8)
    return {
        "coefficients": bell_draw(streams_of[0], (VT, S, A, A), 1.0, 6.0, ((0, 32),)),
        "send_tile": touch_ends(jax.random.randint(streams_of[1], (N_DEV, N_DEV), 0, V_DEV), jax.random.fold_in(streams_of[1], 1), 0, V_DEV - 1).astype(jnp.int32),
        "slot_external": touch_ends(ranked(streams_of[2], (N_DEV, N_DEV), E_DEV, 2), jax.random.fold_in(streams_of[2], 3), 0, E_DEV - 1).astype(jnp.int32),
        "slot_pairs": touch_ends(jax.random.randint(streams_of[3], (N_DEV, N_DEV, J), 0, P_SIZE), jax.random.fold_in(streams_of[3], 1), 0, P_SIZE - 1).astype(jnp.int32),
        "factor_alpha": bell_draw(streams_of[4], (P_SIZE, A, A), A ** -0.5, 0.5),
        "factor_beta": bell_draw(streams_of[5], (P_SIZE, A, A), A ** -0.5, 0.5),
        "denominators": jnp.clip(jnp.exp(math.log(32.0) - 2.0794415 * jax.random.uniform(streams_of[6], (ET, S, A, A), jnp.float32) ** shard_levels(streams_of[6], (ET, S, A, A), ((0, 32),), -0.2, 0.2)), 4.0, 32.0),
    }


def pair_forward(slot_tiles, pair_rows, factor_alpha, factor_beta):
    left_factor = factor_alpha[pair_rows].astype(jnp.float32)
    right_factor = factor_beta[pair_rows].astype(jnp.float32)
    half_product = jnp.einsum('njab,nsac->njsbc', left_factor, slot_tiles.astype(jnp.float32), precision=lax.Precision.HIGHEST).astype(jnp.bfloat16)
    half_product = lax.optimization_barrier(half_product).astype(jnp.float32)
    return jnp.einsum('njsbc,njcd->nsbd', half_product, right_factor, precision=lax.Precision.HIGHEST).astype(jnp.bfloat16)


def pair_adjoint(amplitude_slots, pair_rows, factor_alpha, factor_beta):
    left_factor = factor_alpha[pair_rows].astype(jnp.float32)
    right_factor = factor_beta[pair_rows].astype(jnp.float32)
    half_product = jnp.einsum('njab,nsbd->njsad', left_factor, amplitude_slots.astype(jnp.float32), precision=lax.Precision.HIGHEST).astype(jnp.bfloat16)
    half_product = lax.optimization_barrier(half_product).astype(jnp.float32)
    return jnp.einsum('njsad,njcd->nsac', half_product, right_factor, precision=lax.Precision.HIGHEST).astype(jnp.bfloat16)


def reference(coefficients, send_tile, slot_external, slot_pairs, factor_alpha, factor_beta, denominators):
    by_owner = coefficients.reshape(N_DEV, V_DEV, S, A, A)
    owners = jnp.arange(N_DEV, dtype=jnp.int32)
    external_range = jnp.arange(E_DEV, dtype=jnp.int32)
    tile_range = jnp.arange(V_DEV, dtype=jnp.int32)

    def forward(receiver):
        slot_tiles = by_owner[owners, send_tile[:, receiver]]
        coupling = pair_forward(slot_tiles, slot_pairs[receiver], factor_alpha, factor_beta)
        onehot = (slot_external[receiver][:, None] == external_range[None, :]).astype(jnp.float32)
        return jnp.einsum('ne,nsbd->esbd', onehot, coupling.astype(jnp.float32), precision=lax.Precision.HIGHEST)

    sigma_sum = lax.map(forward, owners).reshape(E_DEV * N_DEV, S, A, A)
    amplitudes = (sigma_sum / denominators).astype(jnp.bfloat16)
    gram = jnp.einsum('esbd,etbd->st', sigma_sum, amplitudes.astype(jnp.float32), precision=lax.Precision.HIGHEST) / (E_DEV * N_DEV * A * A)
    by_device = amplitudes.reshape(N_DEV, E_DEV, S, A, A)

    def backward(dressing_sum, receiver):
        amplitude_slots = by_device[receiver][slot_external[receiver]]
        partial_value = pair_adjoint(amplitude_slots, slot_pairs[receiver], factor_alpha, factor_beta)
        onehot = (send_tile[:, receiver][:, None] == tile_range[None, :]).astype(jnp.float32)
        return dressing_sum + onehot[:, :, None, None, None] * partial_value.astype(jnp.float32)[:, None], None

    dressing_sum, _ = lax.scan(backward, jnp.zeros((N_DEV, V_DEV, S, A, A), jnp.float32), owners)
    return amplitudes, dressing_sum.reshape(V_DEV * N_DEV, S, A, A), gram
```

```python
import functools

import jax
import jax.numpy as jnp
from jax import lax
from jax.experimental import pallas as pl
from jax.experimental.pallas import tpu as pltpu
from jax.sharding import PartitionSpec as P


CORE = 1
AXES = (2, 4)
PLANE = 8


def swap(value, distance):
    count = lax.axis_size("dev")
    return lax.ppermute(value, "dev", [(i, i ^ distance) for i in range(count)])


def gathered(rows):
    distance = 1
    while distance < lax.axis_size("dev"):
        rows = jnp.concatenate([rows, swap(rows, distance)], axis=0)
        distance *= 2
    return rows


def pair_kernel(sizes, forward, place, table, *refs):
    count, planes, tiles, externals, pairs, slots_in, half_out = sizes
    buffers = refs[:4]
    left, right, keep, send, stage, total, arrived = refs[4:]
    copies = [
        pltpu.make_async_copy(buffers[b], stage.at[b], arrived.at[b]) for b in range(4)
    ]
    for copy in copies:
        copy.start()
    keep[...] = jnp.zeros_like(keep)
    total[...] = jnp.zeros_like(total)
    me, across, along = place[0], place[1], place[2]
    side = left.shape[1]
    unroll = min(planes, 4)

    def connection(b, plane, far):
        if forward:
            owner = (plane * PLANE) ^ ((b // 2) * across) ^ (b % 2)
            receiver = far * along
        else:
            owner = (plane * PLANE) ^ (far * across)
            receiver = ((b % 2) * along) ^ (b // 2)
        tile = table[owner, me ^ receiver]
        external = table[receiver, count + (me ^ owner)]
        first = 2 * count + pairs * (me ^ owner)
        picks = [table[receiver, first + j] for j in range(pairs)]
        source = plane * tiles + tile if forward else external
        block = stage[b, source]
        stacked = jnp.concatenate([left[p] for p in picks], axis=0)
        half = jnp.dot(stacked, block, preferred_element_type=jnp.float32).astype(jnp.bfloat16)
        spread = jnp.concatenate([half[j * side : (j + 1) * side] for j in range(pairs)], axis=1)
        factors = jnp.concatenate([right[p] for p in picks], axis=0)
        value = jnp.dot(spread, factors, preferred_element_type=jnp.float32)
        value = value.astype(jnp.bfloat16).astype(jnp.float32)
        out = total if far else keep
        slot = external if forward else plane * tiles + tile
        out[slot] = out[slot] + value

    def group(step, carried):
        b, base = step // (planes // unroll), (step % (planes // unroll)) * unroll
        for far in (1, 0):
            for k in range(unroll):
                connection(b, base + k, far)
        return carried

    for b in range(4):
        copies[b].wait()
    lax.fori_loop(0, 4 * (planes // unroll), group, 0)
    send[...] = total[...].astype(send.dtype)


def pair_call(sizes, forward, place, table, buffers, left, right):
    half_out, side = sizes[-1], left.shape[1]
    vmem = pl.BlockSpec(memory_space=pltpu.VMEM)
    smem = pl.BlockSpec(memory_space=pltpu.SMEM)
    slots = buffers[0].shape[0]
    return pl.pallas_call(
        functools.partial(pair_kernel, sizes, forward),
        out_shape=(
            jax.ShapeDtypeStruct((half_out, side, side), jnp.float32),
            jax.ShapeDtypeStruct((half_out, side, side), jnp.bfloat16),
        ),
        in_specs=[smem, smem] + [pl.BlockSpec(memory_space=pl.ANY)] * 4 + [vmem, vmem],
        out_specs=(vmem, vmem),
        scratch_shapes=[
            pltpu.VMEM((4, slots, side, side), jnp.bfloat16),
            pltpu.VMEM((half_out, side, side), jnp.float32),
            pltpu.SemaphoreType.DMA((4,)),
        ],
        compiler_params=pltpu.CompilerParams(vmem_limit_bytes=40 << 20),
        name="forward_pairs" if forward else "backward_pairs",
    )(place, table, *buffers, left, right)


def gram_kernel(states, *refs):
    sigmas, amplitudes, out = refs[:states], refs[states : 2 * states], refs[-1]
    rows, side = sigmas[0].shape[0], sigmas[0].shape[1]
    out[...] = jnp.zeros_like(out)

    def step(i, carried):
        values = [amplitudes[t][i].astype(jnp.float32) for t in range(states)]
        for s in range(states):
            sigma = sigmas[s][i]
            for t in range(states):
                product = (sigma * values[t]).reshape(side // 8, 8, side).sum(axis=0)
                out[s * states + t] = out[s * states + t] + product
        return carried

    lax.fori_loop(0, rows, step, 0)


def gram_call(sigmas, amplitudes):
    states, side = len(sigmas), sigmas[0].shape[1]
    vmem = pl.BlockSpec(memory_space=pltpu.VMEM)
    sums = pl.pallas_call(
        functools.partial(gram_kernel, states),
        out_shape=jax.ShapeDtypeStruct((states * states, 8, side), jnp.float32),
        in_specs=[vmem] * (2 * states),
        out_specs=vmem,
        compiler_params=pltpu.CompilerParams(vmem_limit_bytes=20 << 20),
        name="gram_sums",
    )(*sigmas, *amplitudes)
    return sums.sum(axis=(1, 2)).reshape(states, states)


def per_device(
    coefficients, send_tile, slot_external, slot_pairs, factor_alpha, factor_beta, denominators
):
    count = lax.axis_size("dev")
    planes = count // PLANE
    tiles, states, side = coefficients.shape[0], coefficients.shape[1], coefficients.shape[2]
    externals, pairs = denominators.shape[0], slot_pairs.shape[2]
    me = lax.axis_index("dev").astype(jnp.int32)
    table = gathered(
        jnp.concatenate([send_tile, slot_external, slot_pairs.reshape(1, -1)], axis=1)
    )
    alpha_turned = factor_alpha.swapaxes(1, 2)
    beta_turned = factor_beta.swapaxes(1, 2)
    forward_sizes = (count, planes, tiles, externals, pairs, planes * tiles, externals)
    backward_sizes = (count, planes, tiles, externals, pairs, externals, planes * tiles)
    sigmas, amplitudes, dressings = [], [], []
    for s in range(states):
        across, along = AXES if s % 2 == 0 else AXES[::-1]
        place = jnp.stack([me, jnp.int32(across), jnp.int32(along)])
        own = coefficients[:, s]
        column = jnp.concatenate(
            [own] + [swap(own, k * PLANE) for k in range(1, planes)], axis=0
        )
        beside = swap(column, across)
        buffers = (column, swap(column, CORE), beside, swap(beside, CORE))
        keep, send = pair_call(
            forward_sizes, True, place, table, buffers, alpha_turned, factor_beta
        )
        sigma = keep + swap(send, along).astype(jnp.float32)
        amplitude = (sigma / denominators[:, s]).astype(jnp.bfloat16)
        sigmas.append(sigma)
        amplitudes.append(amplitude)
        beyond = swap(amplitude, along)
        buffers = (amplitude, beyond, swap(amplitude, CORE), swap(beyond, CORE))
        keep, send = pair_call(
            backward_sizes, False, place, table, buffers, factor_alpha, beta_turned
        )
        part = (keep + swap(send, across).astype(jnp.float32)).reshape(
            planes, tiles, side, side
        )
        dressing = part[0]
        for k in range(1, planes):
            dressing = dressing + swap(part[k].astype(jnp.bfloat16), k * PLANE).astype(
                jnp.float32
            )
        dressings.append(dressing)
    total_cells = count * externals * side * side
    gram = gram_call(sigmas, amplitudes) / total_cells
    distance = 1
    while distance < count:
        gram = gram + swap(gram, distance)
        distance *= 2
    return jnp.stack(amplitudes, axis=1), jnp.stack(dressings, axis=1), gram


def solution(mesh):
    return jax.shard_map(
        per_device,
        mesh=mesh,
        in_specs=(
            P("dev", None, None, None),
            P("dev", None),
            P("dev", None),
            P("dev", None, None),
            P(),
            P(),
            P("dev", None, None, None),
        ),
        out_specs=(P("dev", None, None, None), P("dev", None, None, None), P()),
        check_vma=False,
    )
```

```python
import functools

import jax
import jax.numpy as jnp
from jax import lax
from jax.experimental import pallas as pl
from jax.experimental.pallas import tpu as pltpu
from jax.sharding import PartitionSpec as P


CORE = 1
AXES = (2, 4)
PLANE = 8


def swap(value, distance):
    count = lax.axis_size("dev")
    return lax.ppermute(value, "dev", [(i, i ^ distance) for i in range(count)])


def gathered(row):
    planes = lax.axis_size("dev") // PLANE
    rows = [row] + [swap(row, k * PLANE) for k in range(1, planes)]
    rows = jnp.stack(rows)
    distance = 1
    while distance < PLANE:
        rows = jnp.concatenate([rows, swap(rows, distance)], axis=1)
        distance = 2 * distance
    return rows.reshape(-1, row.shape[1])


def tree_sum(values):
    while len(values) > 1:
        values = [a + b for a, b in zip(values[::2], values[1::2], strict=True)]
    return values[0]


def room(scratch):
    return pltpu.CompilerParams(vmem_limit_bytes=scratch + (4 << 20))


def sigma_kernel(s, keep, arrived, denominators, *refs):
    sigma, amplitude, out, done = refs[-4:]

    def step(i, carried):
        value = keep[i] + arrived[i].astype(jnp.float32)
        sigma[i] = value
        amplitude[i] = (value / denominators[i]).astype(jnp.bfloat16)
        return carried

    lax.fori_loop(0, keep.shape[0], step, 0)
    copy = pltpu.make_async_copy(amplitude, out.at[:, s], done)
    copy.start()
    copy.wait()


def sigma_call(s, states, keep, arrived, denominators, so_far):
    vmem, anywhere = pl.BlockSpec(memory_space=pltpu.VMEM), pl.BlockSpec(memory_space=pl.ANY)
    shape = keep.shape
    before = () if so_far is None else (so_far,)
    return pl.pallas_call(
        functools.partial(sigma_kernel, s),
        out_shape=(
            jax.ShapeDtypeStruct(shape, jnp.float32),
            jax.ShapeDtypeStruct(shape, jnp.bfloat16),
            jax.ShapeDtypeStruct((shape[0], states) + shape[1:], jnp.bfloat16),
        ),
        in_specs=[vmem] * 3 + [anywhere] * len(before),
        out_specs=(vmem, vmem, anywhere),
        scratch_shapes=[pltpu.SemaphoreType.DMA],
        input_output_aliases={3: 2} if before else {},
        compiler_params=room(0),
    )(keep, arrived, denominators, *before)


def part_kernel(keep, arrived, own, *sent):
    tiles = own.shape[0]

    def step(i, carried):
        own[i] = keep[i] + arrived[i].astype(jnp.float32)
        for k, out in enumerate(sent, 1):
            j = k * tiles + i
            out[i] = (keep[j] + arrived[j].astype(jnp.float32)).astype(jnp.bfloat16)
        return carried

    lax.fori_loop(0, tiles, step, 0)


def part_call(planes, keep, arrived):
    vmem = pl.BlockSpec(memory_space=pltpu.VMEM)
    shape = (keep.shape[0] // planes,) + keep.shape[1:]
    return pl.pallas_call(
        part_kernel,
        out_shape=[jax.ShapeDtypeStruct(shape, jnp.float32)]
        + [jax.ShapeDtypeStruct(shape, jnp.bfloat16)] * (planes - 1),
        in_specs=[vmem, vmem],
        out_specs=[vmem] * planes,
        compiler_params=room(0),
    )(keep, arrived)


def dressing_kernel(s, planes, own, *refs):
    sent, (out, total, done) = refs[: planes - 1], refs[-3:]

    def step(i, carried):
        value = own[i]
        for other in sent:
            value = value + other[i].astype(jnp.float32)
        total[i] = value
        return carried

    lax.fori_loop(0, own.shape[0], step, 0)
    copy = pltpu.make_async_copy(total, out.at[:, s], done)
    copy.start()
    copy.wait()


def dressing_call(s, states, own, sent, so_far):
    vmem, anywhere = pl.BlockSpec(memory_space=pltpu.VMEM), pl.BlockSpec(memory_space=pl.ANY)
    shape, planes = own.shape, len(sent) + 1
    before = () if so_far is None else (so_far,)
    return pl.pallas_call(
        functools.partial(dressing_kernel, s, planes),
        out_shape=jax.ShapeDtypeStruct((shape[0], states) + shape[1:], jnp.float32),
        in_specs=[vmem] * planes + [anywhere] * len(before),
        out_specs=anywhere,
        scratch_shapes=[pltpu.VMEM(shape, jnp.float32), pltpu.SemaphoreType.DMA],
        input_output_aliases={planes: 0} if before else {},
        compiler_params=room(own.size * 4),
    )(own, *sent, *before)


def turn_kernel(a, b, a_out, b_out):
    def step(i, carried):
        a_out[i] = a[i].T
        b_out[i] = b[i].T
        return carried

    lax.fori_loop(0, a.shape[0], step, 0, unroll=4)


def turn_call(a, b):
    vmem = pl.BlockSpec(memory_space=pltpu.VMEM)
    return pl.pallas_call(
        turn_kernel,
        out_shape=(a, b),
        in_specs=[vmem] * 2,
        out_specs=(vmem, vmem),
        compiler_params=room(0),
    )(a, b)


def pair_kernel(sizes, forward, place, table, *refs):
    count, planes, tiles, pairs = sizes
    buffers = refs[:4]
    left, right, keep, send, stage, total, arrived = refs[4:]
    for b in range(4):
        pltpu.make_async_copy(buffers[b], stage.at[b], arrived.at[b]).start()
    keep[...] = jnp.zeros_like(keep)
    total[...] = jnp.zeros_like(total)
    me, across, along = place[0], place[1], place[2]
    side = left.shape[1]
    unroll = min(planes, 4)

    def connection(b, plane, far):
        if forward:
            owner = (plane * PLANE) ^ ((b // 2) * across) ^ (b % 2)
            receiver = far * along
        else:
            owner = (plane * PLANE) ^ (far * across)
            receiver = ((b % 2) * along) ^ (b // 2)
        tile = table[owner, me ^ receiver]
        external = table[receiver, count + (me ^ owner)]
        first = 2 * count + pairs * (me ^ owner)
        picks = [table[receiver, first + j] for j in range(pairs)]
        block = stage[b, plane * tiles + tile if forward else external]
        stacked = jnp.concatenate([left[p] for p in picks], axis=0)
        half = jnp.dot(stacked, block, preferred_element_type=jnp.float32).astype(jnp.bfloat16)
        spread = jnp.concatenate([half[j * side : (j + 1) * side] for j in range(pairs)], axis=1)
        factors = jnp.concatenate([right[p] for p in picks], axis=0)
        value = jnp.dot(spread, factors, preferred_element_type=jnp.float32)
        value = value.astype(jnp.bfloat16).astype(jnp.float32)
        out = total if far else keep
        slot = external if forward else plane * tiles + tile
        out[slot] = out[slot] + value

    def buffer(b, carried):
        pltpu.make_async_copy(buffers[0], stage.at[b], arrived.at[b]).wait()

        def group(step, inner):
            for far in (1, 0):
                for k in range(unroll):
                    connection(b, step * unroll + k, far)
            return inner

        if planes == unroll:
            group(0, 0)
        else:
            lax.fori_loop(0, planes // unroll, group, 0)
        return carried

    lax.fori_loop(0, 4, buffer, 0)
    send[...] = total[...].astype(send.dtype)


def pair_call(sizes, forward, slots_out, place, table, buffers, left, right):
    side, slots = left.shape[1], buffers[0].shape[0]
    vmem = pl.BlockSpec(memory_space=pltpu.VMEM)
    smem = pl.BlockSpec(memory_space=pltpu.SMEM)
    return pl.pallas_call(
        functools.partial(pair_kernel, sizes, forward),
        out_shape=(
            jax.ShapeDtypeStruct((slots_out, side, side), jnp.float32),
            jax.ShapeDtypeStruct((slots_out, side, side), jnp.bfloat16),
        ),
        in_specs=[smem, smem] + [pl.BlockSpec(memory_space=pl.ANY)] * 4 + [vmem, vmem],
        out_specs=(vmem, vmem),
        scratch_shapes=[
            pltpu.VMEM((4, slots, side, side), jnp.bfloat16),
            pltpu.VMEM((slots_out, side, side), jnp.float32),
            pltpu.SemaphoreType.DMA((4,)),
        ],
        compiler_params=room(4 * slots * side * side * 2 + slots_out * side * side * 4),
        name="forward_pairs" if forward else "backward_pairs",
    )(place, table, *buffers, left, right)


def gram_kernel(states, *refs):
    sigmas, amplitudes, out = refs[:states], refs[states : 2 * states], refs[-1]
    rows, side = sigmas[0].shape[0], sigmas[0].shape[1]
    out[...] = jnp.zeros_like(out)

    def step(i, carried):
        values = [amplitudes[t][i].astype(jnp.float32) for t in range(states)]
        for s in range(states):
            sigma = sigmas[s][i]
            for t in range(states):
                product = (sigma * values[t]).reshape(side // 8, 8, side).sum(axis=0)
                out[s * states + t] = out[s * states + t] + product
        return carried

    lax.fori_loop(0, rows, step, 0)


def gram_call(sigmas, amplitudes):
    states, side = len(sigmas), sigmas[0].shape[1]
    vmem = pl.BlockSpec(memory_space=pltpu.VMEM)
    sums = pl.pallas_call(
        functools.partial(gram_kernel, states),
        out_shape=jax.ShapeDtypeStruct((states * states, 8, side), jnp.float32),
        in_specs=[vmem] * (2 * states),
        out_specs=vmem,
        compiler_params=room(0),
    )(*sigmas, *amplitudes)
    return sums.sum(axis=(1, 2)).reshape(states, states)


def per_device(
    coefficients, send_tile, slot_external, slot_pairs, factor_alpha, factor_beta, denominators
):
    count = lax.axis_size("dev")
    planes = count // PLANE
    tiles, states, side = coefficients.shape[0], coefficients.shape[1], coefficients.shape[2]
    externals, pairs = denominators.shape[0], slot_pairs.shape[2]
    me = lax.axis_index("dev").astype(jnp.int32)
    table = gathered(
        jnp.concatenate([send_tile, slot_external, slot_pairs.reshape(1, -1)], axis=1)
    )
    alpha_turned, beta_turned = turn_call(factor_alpha, factor_beta)
    sizes = (count, planes, tiles, pairs)
    sigmas, amplitudes, all_amplitudes, dressing = [], [], None, None
    for s in range(states):
        across, along = AXES if s % 2 == 0 else AXES[::-1]
        place = jnp.stack([me, jnp.int32(across), jnp.int32(along)])
        own = coefficients[:, s]
        parts = [own] + [swap(own, k * PLANE) for k in range(1, planes)]
        column = jnp.concatenate(parts, axis=0)
        beside = swap(column, across)
        buffers = (column, swap(column, CORE), beside, swap(beside, CORE))
        keep, send = pair_call(
            sizes, True, externals, place, table, buffers, alpha_turned, factor_beta
        )
        arrived = swap(send, along)
        sigma, amplitude, all_amplitudes = sigma_call(
            s, states, keep, arrived, denominators[:, s], all_amplitudes
        )
        sigmas.append(sigma)
        amplitudes.append(amplitude)
        beyond = swap(amplitude, along)
        buffers = (amplitude, beyond, swap(amplitude, CORE), swap(beyond, CORE))
        keep, send = pair_call(
            sizes, False, planes * tiles, place, table, buffers, factor_alpha, beta_turned
        )
        arrived = swap(send, across)
        own, *sent = part_call(planes, keep, arrived)
        sent = [swap(value, k * PLANE) for k, value in enumerate(sent, 1)]
        dressing = dressing_call(s, states, own, sent, dressing)
    total_cells = count * externals * side * side
    gram = gram_call(sigmas, amplitudes) / total_cells
    gram = tree_sum([gram] + [swap(gram, k * PLANE) for k in range(1, planes)])
    distance = 1
    while distance < PLANE:
        gram = gram + swap(gram, distance)
        distance = 2 * distance
    return all_amplitudes, dressing, gram


def solution(mesh):
    return jax.shard_map(
        per_device,
        mesh=mesh,
        in_specs=(
            P("dev", None, None, None),
            P("dev", None),
            P("dev", None),
            P("dev", None, None),
            P(),
            P(),
            P("dev", None, None, None),
        ),
        out_specs=(P("dev", None, None, None), P("dev", None, None, None), P()),
        check_vma=False,
    )
```
